256 devices in a mesh: seq: 128 (over z, x, y), tp: 2 (over core).
Axes of the slice: x: 4, y: 4, z: 8, core: 2. Of those that a mesh axis runs over, the one named last changes fastest.
Arguments:
- latent: bfloat16 [128, 8, 32, 128], P(None, 'tp', None, 'seq'), may hold values from -8 to 8
- conv_weight: bfloat16 [3, 3, 3, 32, 128], replicated, may hold values from -0.21875 to 0.21875
- conv_bias: float32 [128], replicated, may hold values from -4 to 4
- proj_weight: bfloat16 [128, 32], replicated, may hold values from -0.5 to 0.5
- embed_weight: bfloat16 [32, 2240], replicated, may hold values from -1 to 1
- embed_bias: float32 [2240], replicated, may hold values from -3 to 3
- qkv_weight: bfloat16 [3, 2240, 1120], P(None, None, 'tp'), may hold values from -0.125 to 0.125
Outputs:
- attended: bfloat16 [131072, 1120], P('seq', 'tp')
The draws below stay inside these ranges and needn't reach their ends.
All inputs are finite; a program needn't handle non-finite values.
Results may differ from the reference program's by a relative error of at most 0.0034.
Values may be sent and summed in bfloat16 or wider, within the bound.
A program may use at most 128 MiB of HBM per device.

```python
import jax
import jax.numpy as jnp
from jax import lax

D = 2240
HEADS = 10
DH = 112
C_IN = 32
C_MID = 128
H = 128
W = 8
NF = 128
FRAMES = 128


def draw_latent(key, part):
    key_offset = jax.random.fold_in(key, 11)
    key_noise = jax.random.fold_in(key, 12)
    position = (jnp.arange(NF) % FRAMES).astype(jnp.float32) / FRAMES
    amplitude = 1.0 + 2.0 * position
    offset = jax.random.normal(key_offset, (C_IN, NF), jnp.float32)
    noise = jax.random.normal(key_noise, (H, W, C_IN, NF), jnp.float32)
    values = amplitude * (0.8 * offset[None, None] + 0.6 * noise)
    return jnp.clip(values, -8.0, 8.0).astype(jnp.bfloat16)


def levels(key, dims, cuts, least, top_value):
    loudness, own = 1.0, jax.random.fold_in(key, 6)
    for dim, blocks in cuts:
        steps = jnp.exp(jax.random.uniform(jax.random.fold_in(own, dim), (blocks,), jnp.float32, least / len(cuts), top_value / len(cuts)))
        loudness = loudness * jnp.repeat(steps, dims[dim] // blocks).reshape([-1 if axis == dim else 1 for axis in range(len(dims))])
    return loudness


def scatter_about(own_key, shape, spread, reach, cuts=(), kind=jnp.bfloat16):
    factor_of = levels(own_key, shape, cuts, -0.22, 0.18) if cuts else 1.0
    array = jax.random.normal(own_key, shape, jnp.float32) * spread * factor_of
    return jnp.minimum(jnp.maximum(array, -reach), reach).astype(kind)


def setup_inputs(seed: int = 0) -> dict:
    streams_of = jax.random.split(jax.random.key(seed), 8)
    return {
        "latent": draw_latent(jax.random.fold_in(streams_of[7], 71), 0),
        "conv_weight": scatter_about(streams_of[1], (3, 3, 3, C_IN, C_MID), (27 * C_IN) ** -0.5, 0.21875),
        "conv_bias": scatter_about(streams_of[2], (C_MID,), 1.0, 4.0, (), jnp.float32),
        "proj_weight": scatter_about(streams_of[3], (C_MID, C_IN), C_MID ** -0.5, 0.5),
        "embed_weight": scatter_about(streams_of[4], (C_IN, D), C_IN ** -0.5, 1.0),
        "embed_bias": scatter_about(streams_of[5], (D,), 0.5, 3.0, (), jnp.float32),
        "qkv_weight": scatter_about(streams_of[6], (3, D, HEADS * DH), D ** -0.5, 0.125, ((2, 2),)),
    }


epsilon = 1e-6


def conv_block(extended, latent, conv_weight, conv_bias, proj_weight, position, per_clip):
    height = extended.shape[0] - 2
    width_dev = extended.shape[1] - 2
    nframes = extended.shape[3] - 2
    pieces = []
    for frame_step in range(3):
        window = extended[:, :, :, frame_step:frame_step + nframes]
        if frame_step == 0:
            window = window * (position >= 1).astype(window.dtype)
        if frame_step == 2:
            window = window * (position <= per_clip - 2).astype(window.dtype)
        for row_step in range(3):
            for col_step in range(3):
                pieces.append(window[row_step:row_step + height, col_step:col_step + width_dev])
    patches = jnp.concatenate(pieces, axis=2)
    kernel = conv_weight.reshape(-1, conv_weight.shape[-1])
    conv = jnp.einsum("rckf,ko->rcof", patches.astype(jnp.float32), kernel.astype(jnp.float32))
    conv = conv + conv_bias[None, None, :, None]
    act = jax.nn.silu(conv).astype(jnp.bfloat16)
    mixed = jnp.einsum("rcof,oi->rcif", act.astype(jnp.float32), proj_weight.astype(jnp.float32))
    return (mixed + latent.astype(jnp.float32)).astype(jnp.bfloat16)


def reference(latent, conv_weight, conv_bias, proj_weight, embed_weight, embed_bias, qkv_weight):
    extended = jnp.pad(latent, ((1, 1), (1, 1), (0, 0), (1, 1)))
    position = jnp.arange(NF, dtype=jnp.int32) % FRAMES
    mixed = conv_block(extended, latent, conv_weight, conv_bias, proj_weight, position, FRAMES)

    def frame_turn(carry, frame):
        state, norm = carry
        fresh = (frame % FRAMES) == 0
        state = jnp.where(fresh, jnp.zeros_like(state), state)
        norm = jnp.where(fresh, jnp.zeros_like(norm), norm)
        slab = lax.dynamic_index_in_dim(mixed, frame, 3, keepdims=False)
        embedded = jnp.einsum("hwc,cd->hwd", slab.astype(jnp.float32), embed_weight.astype(jnp.float32))
        embedded = (embedded + embed_bias).astype(jnp.bfloat16).reshape(-1, D)
        projected = jnp.einsum("td,sde->ste", embedded.astype(jnp.float32), qkv_weight.astype(jnp.float32))
        projected = projected.astype(jnp.bfloat16).astype(jnp.float32)
        queries = jax.nn.relu(projected[0]).reshape(-1, HEADS, DH)
        keys = jax.nn.relu(projected[1]).reshape(-1, HEADS, DH)
        values = projected[2].reshape(-1, HEADS, DH)
        state = state + jnp.einsum("thi,thj->hij", keys, values, precision=lax.Precision.HIGHEST)
        norm = norm + jnp.sum(keys, axis=0)
        numer = jnp.einsum("thi,hij->thj", queries, state, precision=lax.Precision.HIGHEST)
        denom = jnp.einsum("thi,hi->th", queries, norm, precision=lax.Precision.HIGHEST) + epsilon
        result = (numer / denom[:, :, None]).astype(jnp.bfloat16).reshape(-1, HEADS * DH)
        return (state, norm), result

    start = (jnp.zeros((HEADS, DH, DH), jnp.float32), jnp.zeros((HEADS, DH), jnp.float32))
    carry, outputs = lax.scan(frame_turn, start, jnp.arange(NF, dtype=jnp.int32))
    return outputs.reshape(-1, HEADS * DH)
```

```python
import functools

import jax
import jax.numpy as jnp
from jax import lax
from jax.experimental import pallas as pl
from jax.experimental.pallas import tpu as pltpu
from jax.sharding import PartitionSpec as P

MESH = pl.DeviceIdType.MESH
F32 = jnp.float32
BF16 = jnp.bfloat16
DH = 112
HEADS = 5
PLANE = 16
DEPTH = 8
OWNERS = 11
NF = PLANE * DEPTH
TOK = 1024
EPS = 1e-6


def nt(a, b):
    return lax.dot_general(a, b, (((1,), (1,)), ((), ())), preferred_element_type=F32)


def nn(a, b):
    return lax.dot_general(a, b, (((1,), (0,)), ((), ())), preferred_element_type=F32)


def three(value):
    hi = value.astype(BF16).astype(F32)
    rest = value - hi
    mid = rest.astype(BF16).astype(F32)
    return hi, mid, (rest - mid).astype(BF16).astype(F32)


def rows_of(parts, rows, width):
    index = lax.broadcasted_iota(jnp.int32, (rows, width), 0)
    out = jnp.zeros((rows, width), F32)
    for i, part in enumerate(parts):
        out = jnp.where(index == i, jnp.broadcast_to(part, (rows, width)), out)
    return out


def kernel(
    lat, cw, cb, pw, ew, eb, w_hbm, out_hbm,
    frames, w, ea, g, cwt, pat, maug, qaug, perm, kt, qt, sx, r1, rz, tz, p3, px, stage,
    hs, hr, ws, s1, v1, s2, v2, s3, v3, os_,
):
    f = lax.axis_index("seq")
    t = lax.axis_index("tp")
    z, p = f // PLANE, f % PLANE
    o = 1 - t
    nxt, prv = (f + 1) % NF, (f + NF - 1) % NF

    barrier = pltpu.get_barrier_semaphore()

    def greet(seq, core):
        pl.semaphore_signal(barrier, inc=1, device_id=(seq, core), device_id_type=MESH)

    greet(f, o)
    for seq in (nxt, prv):
        greet(seq, t)
        greet(seq, o)

    def greet_plane(k, c):
        greet(z * PLANE + (p + k) % PLANE, t)
        return c

    lax.fori_loop(1, PLANE, greet_plane, 0)

    def greet_depth(k, c):
        greet(((z + k) % DEPTH) * PLANE + p, t)
        return c

    lax.fori_loop(1, DEPTH, greet_depth, 0)

    def wcopy(i):
        return pltpu.make_async_copy(w_hbm.at[i], w.at[i], ws.at[i])

    for i in range(3):
        wcopy(i).start()

    frames[1, t] = lat[...]

    width = ew.shape[1]
    bias = three(eb[...])
    ea[0:32] = ew[...]
    ea[32:64] = ew[...]
    ea[64:80] = rows_of(bias + bias, 16, width).astype(BF16)
    ea[80:128] = jnp.zeros((48, width), BF16)

    wide = jnp.concatenate([cw[...].astype(F32), rows_of(three(cb[...]), 32, 128)], axis=0)
    cwt[...] = wide.T.astype(BF16)
    pat[864:896] = jnp.ones((32, TOK), BF16)

    pl.semaphore_wait(barrier, 5 + PLANE - 1 + DEPTH - 1)

    sends = []
    for i, (slot, seq, core) in enumerate(((0, nxt, t), (2, prv, t), (0, nxt, o), (2, prv, o), (1, f, o))):
        copy = pltpu.make_async_remote_copy(
            src_ref=lat, dst_ref=frames.at[slot, t], send_sem=hs.at[i], recv_sem=hr.at[slot, t],
            device_id=(seq, core), device_id_type=MESH)
        copy.start()
        sends.append(copy)

    lane = lax.broadcasted_iota(jnp.int32, (HEADS * DH, 128), 1)
    low = ((lane >= 32) & (lane < 64)) | (lane >= 67)

    def fold(i, c):
        wcopy(i).wait()
        full = nt(w[i], ea[...])
        hi = full.astype(BF16).astype(F32)
        g[i] = jnp.where(low, full - hi, hi).astype(BF16)
        return c

    lax.fori_loop(0, 3, fold, 0)

    def fill(i, c):
        target = lax.broadcasted_iota(jnp.int32, (128, TOK), 1)
        source = lax.broadcasted_iota(jnp.int32, (128, TOK), 0)
        hit = ((target & 7) == i) & ((target >> 3) == source)
        perm[pl.ds(pl.multiple_of(i * 128, 128), 128)] = jnp.where(hit, 1.0, 0.0).astype(BF16)
        return c

    lax.fori_loop(0, 8, fill, 0)
    sx[...] = jnp.zeros_like(sx)

    def arrived(slot, core, i):
        pltpu.make_async_remote_copy(
            src_ref=lat, dst_ref=frames.at[slot, core], send_sem=hs.at[i], recv_sem=hr.at[slot, core],
            device_id=(f, o), device_id_type=MESH).wait_recv()

    arrived(1, o, 4)
    for slot in (0, 2):
        arrived(slot, t, 0)
        arrived(slot, o, 0)

    row = lax.broadcasted_iota(jnp.int32, (32, TOK), 1) & 127
    none = jnp.zeros((32, 128), BF16)
    here = None
    for a in range(3):
        x = jnp.concatenate([frames[a, c // 4, c % 4] for c in range(8)], axis=1).astype(F32)
        if a == 0:
            x = jnp.where(f > 0, x, 0.0)
        if a == 2:
            x = jnp.where(f < NF - 1, x, 0.0)
        if a == 1:
            here = x
        shifted = (
            jnp.where(row == 0, 0.0, pltpu.roll(x, 1, 1)),
            x,
            jnp.where(row == 127, 0.0, pltpu.roll(x, TOK - 1, 1)),
        )
        for b in range(3):
            y = shifted[b].astype(BF16)
            base = (a * 3 + b) * 96
            pat[base : base + 32] = jnp.concatenate([none, y[:, : TOK - 128]], axis=1)
            pat[base + 32 : base + 64] = y
            pat[base + 64 : base + 96] = jnp.concatenate([y[:, 128:], none], axis=1)
    conv = nn(cwt[...], pat[...])
    act = (conv / (1.0 + jnp.exp(-conv))).astype(BF16)
    mixed = (nn(pw[...], act) + here).astype(BF16)
    maug[0:32] = mixed
    maug[32:64] = mixed
    maug[64:80] = jnp.ones((16, TOK), BF16)
    maug[80:128] = jnp.zeros((48, TOK), BF16)

    kt[...] = jnp.maximum(nn(g[1], maug[...]), 0.0).astype(BF16)
    plus = maug[32:80]
    for h in range(HEADS):
        s = nt(plus, kt[h * DH : (h + 1) * DH])
        sx[2 * h, :, 0:DH] = s[0:16]
        sx[2 * h + 1, :, 0:DH] = s[16:32]
        sx[10, h : h + 1, 0:DH] = s[32:33]

    def one(k, c):
        q = (p + k) % PLANE

        @pl.when(q < OWNERS)
        def _():
            pltpu.make_async_remote_copy(
                src_ref=sx.at[q], dst_ref=r1.at[p], send_sem=s1.at[k], recv_sem=v1.at[p],
                device_id=(z * PLANE + q, t), device_id_type=MESH).start()

        return c

    lax.fori_loop(1, PLANE, one, 0)

    def queries():
        qaug[...] = nn(maug[...], perm[...]).astype(BF16)
        qt[...] = jnp.maximum(nn(g[0], qaug[...]), 0.0).astype(BF16)

    @pl.when(p < OWNERS)
    def _():
        r1[p] = sx[p]

        def got(k, c):
            q = (p + k) % PLANE
            pltpu.make_async_remote_copy(
                src_ref=sx.at[0], dst_ref=r1.at[q], send_sem=s1.at[0], recv_sem=v1.at[q],
                device_id=(f, o), device_id_type=MESH).wait_recv()
            return c

        lax.fori_loop(1, PLANE, got, 0)
        total = r1[0]
        for i in range(1, PLANE):
            total = total + r1[i]
        tz[...] = total

        def two(k, c):
            q = (z + k) % DEPTH
            pltpu.make_async_remote_copy(
                src_ref=tz, dst_ref=rz.at[z], send_sem=s2.at[k], recv_sem=v2.at[z],
                device_id=(q * PLANE + p, t), device_id_type=MESH).start()
            return c

        lax.fori_loop(1, DEPTH, two, 0)
        rz[z] = total

    queries()

    @pl.when(p < OWNERS)
    def _():
        def got(k, c):
            q = (z + k) % DEPTH
            pltpu.make_async_remote_copy(
                src_ref=tz, dst_ref=rz.at[q], send_sem=s2.at[0], recv_sem=v2.at[q],
                device_id=(f, o), device_id_type=MESH).wait_recv()
            return c

        lax.fori_loop(1, DEPTH, got, 0)
        run = jnp.zeros((16, 128), F32)
        for i in range(DEPTH - 1):
            run = run + jnp.where(i < z, rz[i], 0.0)
        for i in range(PLANE):
            p3[i] = run
            run = run + r1[i]

        def three_(k, c):
            q = (p + k) % PLANE
            pltpu.make_async_remote_copy(
                src_ref=p3.at[q], dst_ref=px.at[p], send_sem=s3.at[k], recv_sem=v3.at[p],
                device_id=(z * PLANE + q, t), device_id_type=MESH).start()
            return c

        lax.fori_loop(1, PLANE, three_, 0)
        px[p] = p3[p]

    def back(k, c):
        q = (p + k) % PLANE

        @pl.when(q < OWNERS)
        def _():
            pltpu.make_async_remote_copy(
                src_ref=p3.at[0], dst_ref=px.at[q], send_sem=s3.at[0], recv_sem=v3.at[q],
                device_id=(f, o), device_id_type=MESH).wait_recv()

        return c

    lax.fori_loop(1, PLANE, back, 0)

    norms = px[10] + sx[10]
    for h in range(HEADS):
        s = jnp.concatenate([
            px[2 * h] + sx[2 * h], px[2 * h + 1] + sx[2 * h + 1],
            jnp.broadcast_to(norms[h : h + 1], (16, 128))], axis=0)[:, 0:DH]
        hi = s.astype(BF16)
        lo = (s - hi.astype(F32)).astype(BF16)
        both = nn(jnp.concatenate([hi, lo], axis=0), qt[h * DH : (h + 1) * DH])
        n = both[0:48] + both[48:96]
        den = n[32:33]
        inv = 1.0 / (den + EPS)
        r = n[0:32] * jnp.broadcast_to(inv, (32, TOK))
        ratio = jnp.broadcast_to(den * inv, (16, TOK))
        rows = jnp.concatenate([r, r, ratio], axis=0)
        top = rows.astype(BF16)
        rest = (rows - top.astype(F32)).astype(BF16)
        gv = g[2, h * DH : (h + 1) * DH, 0:80]
        stage[h] = (nn(gv, top) + nn(gv, rest)).astype(BF16)
        pltpu.make_async_copy(stage.at[h], out_hbm.at[h], os_.at[h]).start()

    for copy in sends:
        copy.wait_send()

    def sent(k, c):
        @pl.when((p + k) % PLANE < OWNERS)
        def _():
            pltpu.make_async_remote_copy(
                src_ref=sx.at[0], dst_ref=r1.at[0], send_sem=s1.at[k], recv_sem=v1.at[0],
                device_id=(f, o), device_id_type=MESH).wait_send()

        @pl.when(p < OWNERS)
        def _():
            pltpu.make_async_remote_copy(
                src_ref=p3.at[0], dst_ref=px.at[0], send_sem=s3.at[k], recv_sem=v3.at[0],
                device_id=(f, o), device_id_type=MESH).wait_send()

        return c

    lax.fori_loop(1, PLANE, sent, 0)

    @pl.when(p < OWNERS)
    def _():
        def gone(k, c):
            pltpu.make_async_remote_copy(
                src_ref=tz, dst_ref=rz.at[0], send_sem=s2.at[k], recv_sem=v2.at[0],
                device_id=(f, o), device_id_type=MESH).wait_send()
            return c

        lax.fori_loop(1, DEPTH, gone, 0)

    for h in range(HEADS):
        pltpu.make_async_copy(stage.at[h], out_hbm.at[h], os_.at[h]).wait()


def per_device(latent, conv_weight, conv_bias, proj_weight, embed_weight, embed_bias, qkv_weight):
    width = embed_weight.shape[1]
    lat = jnp.transpose(latent, (1, 3, 2, 0)).reshape(4, 32, 128)
    vmem, anywhere = pl.BlockSpec(memory_space=pltpu.VMEM), pl.BlockSpec(memory_space=pl.ANY)
    dma, vm = pltpu.SemaphoreType.DMA, pltpu.VMEM
    out = pl.pallas_call(
        kernel,
        out_shape=jax.ShapeDtypeStruct((HEADS, DH, TOK), BF16),
        in_specs=[vmem] * 6 + [anywhere],
        out_specs=anywhere,
        scratch_shapes=[
            vm((3, 2, 4, 32, 128), BF16),
            vm((3, HEADS * DH, width), BF16),
            vm((128, width), BF16),
            vm((3, HEADS * DH, 128), BF16),
            vm((128, 896), BF16),
            vm((896, TOK), BF16),
            vm((128, TOK), BF16),
            vm((128, TOK), BF16),
            vm((TOK, TOK), BF16),
            vm((HEADS * DH, TOK), BF16),
            vm((HEADS * DH, TOK), BF16),
            vm((OWNERS, 16, 128), F32),
            vm((PLANE, 16, 128), F32),
            vm((DEPTH, 16, 128), F32),
            vm((16, 128), F32),
            vm((PLANE, 16, 128), F32),
            vm((OWNERS, 16, 128), F32),
            vm((HEADS, DH, TOK), BF16),
            dma((5,)), dma((3, 2)), dma((3,)),
            dma((PLANE,)), dma((PLANE,)), dma((DEPTH,)), dma((DEPTH,)), dma((PLANE,)), dma((PLANE,)),
            dma((HEADS,)),
        ],
        compiler_params=pltpu.CompilerParams(collective_id=0, has_side_effects=True),
    )(
        lat, conv_weight.reshape(864, 128), conv_bias.reshape(1, 128), jnp.transpose(proj_weight),
        embed_weight, embed_bias.reshape(1, width), jnp.transpose(qkv_weight, (0, 2, 1)),
    )
    return jnp.transpose(out.reshape(HEADS * DH, TOK))


def solution(mesh):
    return jax.shard_map(
        per_device,
        mesh=mesh,
        in_specs=(P(None, "tp", None, "seq"), P(), P(), P(), P(), P(), P(None, None, "tp")),
        out_specs=P("seq", "tp"),
        check_vma=False,
    )
```

```python
import functools

import jax
import jax.numpy as jnp
from jax import lax
from jax.experimental import pallas as pl
from jax.experimental.pallas import tpu as pltpu
from jax.sharding import PartitionSpec as P

MESH = pl.DeviceIdType.MESH
F32 = jnp.float32
BF16 = jnp.bfloat16
DH = 112
HEADS = 5
PLANE = 16
DEPTH = 8
OWNERS = 11
NF = PLANE * DEPTH
TOK = 1024
EPS = 1e-6


def nt(a, b):
    return lax.dot_general(a, b, (((1,), (1,)), ((), ())), preferred_element_type=F32)


def nn(a, b):
    return lax.dot_general(a, b, (((1,), (0,)), ((), ())), preferred_element_type=F32)


def three(value):
    hi = value.astype(BF16).astype(F32)
    rest = value - hi
    mid = rest.astype(BF16).astype(F32)
    return hi, mid, (rest - mid).astype(BF16).astype(F32)


def rows_of(parts, rows, width):
    index = lax.broadcasted_iota(jnp.int32, (rows, width), 0)
    out = jnp.zeros((rows, width), F32)
    for i, part in enumerate(parts):
        out = jnp.where(index == i, jnp.broadcast_to(part, (rows, width)), out)
    return out


def kernel(
    lat_hbm, cw_hbm, cb_hbm, pw_hbm, ew_hbm, eb_hbm, w_hbm, total_out, gv_out, qt,
    lat, cw, cb, pw, eb, frames, w, ea, g, cwt, pat, maug, qaug, perm, kt, sx, r1, rz, tz, p3, px,
    ls, hs, hr, ws, s1, v1, s2, v2, s3, v3, tok, ztok,
):
    f = lax.axis_index("seq")
    t = lax.axis_index("tp")
    z, p = f // PLANE, f % PLANE
    o = 1 - t
    x, y = p // 4, p % 4

    def load(src, dst, i):
        return pltpu.make_async_copy(src, dst, ls.at[i])

    loads = [
        load(lat_hbm, lat, 0), load(eb_hbm, eb, 1), load(ew_hbm, ea.at[0:32], 2), load(ew_hbm, ea.at[32:64], 3),
        load(cw_hbm, cw, 4), load(cb_hbm, cb, 5), load(pw_hbm, pw, 6),
    ]
    for copy in loads:
        copy.start()

    def wcopy(i, half):
        rows = pl.ds(half * 288, 288 - 16 * half)
        return pltpu.make_async_copy(w_hbm.at[i, rows], w.at[i, rows], ws.at[i, half])

    for i in (1, 2, 0):
        for half in range(2):
            wcopy(i, half).start()

    barrier = pltpu.get_barrier_semaphore()

    def near(act):
        for ok, seq in ((y > 0, f - 1), (y < 3, f + 1), (x > 0, f - 4), (x < 3, f + 4)):
            pl.when(ok)(functools.partial(act, seq))

    def ahead(step, act, back=True):
        if back:
            pl.when(z >= step)(functools.partial(act, f - step * PLANE))
        if back != "only":
            pl.when(z < DEPTH - step)(functools.partial(act, f + step * PLANE))

    def at_least(value, least, top):
        return (value + top + 1 - least) // (top + 1)

    around = at_least(y, 1, 3) + at_least(3 - y, 1, 3) + at_least(x, 1, 3) + at_least(3 - x, 1, 3)

    def planes(step):
        return at_least(z, step, 7) + at_least(7 - z, step, 7)

    def signal(sem, seq, core):
        pl.semaphore_signal(sem, inc=1, device_id=(seq, core), device_id_type=MESH)

    signal(barrier, f, o)
    for ok, seq in ((f > 0, f - 1), (f < NF - 1, f + 1)):
        @pl.when(ok)
        def _():
            signal(barrier, seq, t)
            signal(barrier, seq, o)

    near(lambda seq: signal(barrier, seq, t))
    ahead(1, lambda seq: signal(barrier, seq, t))

    loads[0].wait()
    frames[1, t] = lat[...]

    width = ea.shape[1]
    loads[1].wait()
    bias = three(eb[...].reshape(1, width))
    ea[64:80] = rows_of(bias + bias, 16, width).astype(BF16)
    ea[80:128] = jnp.zeros((48, width), BF16)

    loads[4].wait()
    loads[5].wait()
    wide = jnp.concatenate([cw[...].astype(F32), rows_of(three(cb[...]), 32, 128)], axis=0)
    cwt[...] = wide.T.astype(BF16)
    pat[864:896] = jnp.ones((32, TOK), BF16)

    pl.semaphore_wait(barrier, 1 + 2 * at_least(f, 1, NF - 1) + 2 * at_least(NF - 1 - f, 1, NF - 1) + around + planes(1))

    def halo(i):
        slot, step, core = ((1, 0, o), (0, 1, t), (0, 1, o), (2, -1, t), (2, -1, o))[i]
        return pltpu.make_async_remote_copy(
            src_ref=lat, dst_ref=frames.at[slot, t], send_sem=hs.at[i], recv_sem=hr.at[slot, t],
            device_id=((f + step + NF) % NF, core), device_id_type=MESH)

    def halos(act):
        act(halo(0))

        @pl.when(f < NF - 1)
        def _():
            act(halo(1))
            act(halo(2))

        @pl.when(f > 0)
        def _():
            act(halo(3))
            act(halo(4))

    halos(lambda copy: copy.start())
    near(lambda seq: signal(tok.at[0], seq, t))
    ahead(1, lambda seq: signal(ztok.at[0], seq, t))

    lane = lax.broadcasted_iota(jnp.int32, (HEADS * DH, 128), 1)
    low = ((lane >= 32) & (lane < 64)) | (lane >= 67)

    loads[2].wait()
    loads[3].wait()
    loads[6].wait()

    def fold(i, c):
        wcopy(i, 0).wait()
        wcopy(i, 1).wait()
        full = nt(w[i], ea[...])
        hi = full.astype(BF16).astype(F32)
        g[i] = jnp.where(low, full - hi, hi).astype(BF16)
        return c

    fold(1, 0)
    fold(2, 0)
    fold(0, 0)

    pl.semaphore_wait(tok.at[0], around)
    floor = z * PLANE
    signal(tok.at[1], floor + x * 4 + (y + 2) % 4, t)
    signal(tok.at[1], floor + (p + 8) % PLANE, t)
    def fill(i, c):
        target = lax.broadcasted_iota(jnp.int32, (128, TOK), 1)
        source = lax.broadcasted_iota(jnp.int32, (128, TOK), 0)
        hit = ((target & 7) == i) & ((target >> 3) == source)
        perm[pl.ds(pl.multiple_of(i * 128, 128), 128)] = jnp.where(hit, 1.0, 0.0).astype(BF16)
        return c

    lax.fori_loop(0, 8, fill, 0)
    sx[...] = jnp.zeros_like(sx)

    def arrived(slot, core):
        pltpu.make_async_remote_copy(
            src_ref=lat, dst_ref=frames.at[slot, core], send_sem=hs.at[0], recv_sem=hr.at[slot, core],
            device_id=(f, o), device_id_type=MESH).wait_recv()

    arrived(1, o)
    for ok, slot in ((f > 0, 0), (f < NF - 1, 2)):
        @pl.when(ok)
        def _():
            arrived(slot, t)
            arrived(slot, o)

    row = lax.broadcasted_iota(jnp.int32, (32, TOK), 1) & 127
    none = jnp.zeros((32, 128), BF16)
    here = None
    for a in range(3):
        x = jnp.concatenate([frames[a, c // 4, c % 4] for c in range(8)], axis=1).astype(F32)
        if a == 0:
            x = jnp.where(f > 0, x, 0.0)
        if a == 2:
            x = jnp.where(f < NF - 1, x, 0.0)
        if a == 1:
            here = x
        shifted = (
            jnp.where(row == 0, 0.0, pltpu.roll(x, 1, 1)),
            x,
            jnp.where(row == 127, 0.0, pltpu.roll(x, TOK - 1, 1)),
        )
        for b in range(3):
            moved = shifted[b].astype(BF16)
            at = (a * 3 + b) * 96
            pat[at : at + 32] = jnp.concatenate([none, moved[:, : TOK - 128]], axis=1)
            pat[at + 32 : at + 64] = moved
            pat[at + 64 : at + 96] = jnp.concatenate([moved[:, 128:], none], axis=1)
    pl.semaphore_wait(ztok.at[0], planes(1))
    ahead(2, lambda seq: signal(ztok.at[1], seq, t))
    pl.semaphore_wait(tok.at[1], 2)
    for k in range(1, 4):
        signal(tok.at[2], floor + (p + 4 * k) % PLANE, t)
    conv = nn(cwt[...], pat[...])
    act = (conv / (1.0 + jnp.exp(-conv))).astype(BF16)
    mixed = (nn(pw[...], act) + here).astype(BF16)
    maug[0:32] = mixed
    maug[32:64] = mixed
    maug[64:80] = jnp.ones((16, TOK), BF16)
    maug[80:128] = jnp.zeros((48, TOK), BF16)

    kt[...] = jnp.maximum(nn(g[1], maug[...]), 0.0).astype(BF16)
    plus = maug[32:80]
    for h in range(HEADS):
        s = nt(plus, kt[h * DH : (h + 1) * DH])
        sx[2 * h, :, 0:DH] = s[0:16]
        sx[2 * h + 1, :, 0:DH] = s[16:32]
        sx[10, h : h + 1, 0:DH] = s[32:33]

    pl.semaphore_wait(tok.at[2], 3)

    def along(k):
        return pltpu.make_async_remote_copy(
            src_ref=tz, dst_ref=rz.at[z], send_sem=s2.at[k], recv_sem=v2.at[z],
            device_id=((f + k * PLANE) % NF, t), device_id_type=MESH)

    def later(act):
        for k in range(1, DEPTH):
            pl.when(z + k < DEPTH)(functools.partial(act, k))

    def one(k, c):
        q = (p + k) % PLANE

        @pl.when(q < OWNERS)
        def _():
            pltpu.make_async_remote_copy(
                src_ref=sx.at[q], dst_ref=r1.at[p], send_sem=s1.at[k], recv_sem=v1.at[p],
                device_id=(z * PLANE + q, t), device_id_type=MESH).start()

        return c

    lax.fori_loop(1, PLANE, one, 0)

    pl.semaphore_wait(ztok.at[1], planes(2))
    ahead(4, lambda seq: signal(ztok.at[2], seq, t), "only")

    def queries():
        qaug[...] = nn(maug[...], perm[...]).astype(BF16)
        qt[...] = jnp.maximum(nn(g[0], qaug[...]), 0.0).astype(BF16)

    @pl.when(p < OWNERS)
    def _():
        r1[p] = sx[p]

        def got(k, c):
            q = (p + k) % PLANE
            pltpu.make_async_remote_copy(
                src_ref=sx.at[0], dst_ref=r1.at[q], send_sem=s1.at[0], recv_sem=v1.at[q],
                device_id=(f, o), device_id_type=MESH).wait_recv()
            return c

        lax.fori_loop(1, PLANE, got, 0)
        total = r1[0]
        for i in range(1, PLANE):
            total = total + r1[i]
        tz[...] = total
        pl.when(z < 4)(functools.partial(pl.semaphore_wait, ztok.at[2], 1))
        later(lambda k: along(k).start())
        run = jnp.zeros((16, 128), F32)
        for i in range(PLANE):
            p3[i] = run
            run = run + r1[i]

    @pl.when((p >= OWNERS) & (z < 4))
    def _():
        pl.semaphore_wait(ztok.at[2], 1)

    queries()

    @pl.when(p < OWNERS)
    def _():
        def got(k, c):
            @pl.when(k < z)
            def _():
                pltpu.make_async_remote_copy(
                    src_ref=tz, dst_ref=rz.at[k], send_sem=s2.at[0], recv_sem=v2.at[k],
                    device_id=(f, o), device_id_type=MESH).wait_recv()

            return c

        lax.fori_loop(0, DEPTH - 1, got, 0)
        before = jnp.zeros((16, 128), F32)
        for i in range(DEPTH - 1):
            before = before + jnp.where(i < z, rz[i], 0.0)
        for i in range(PLANE):
            p3[i] = p3[i] + before

        def three_(k, c):
            q = (p + k) % PLANE
            pltpu.make_async_remote_copy(
                src_ref=p3.at[q], dst_ref=px.at[p], send_sem=s3.at[k], recv_sem=v3.at[p],
                device_id=(z * PLANE + q, t), device_id_type=MESH).start()
            return c

        lax.fori_loop(1, PLANE, three_, 0)
        px[p] = p3[p]

    def back(k, c):
        q = (p + k) % PLANE

        @pl.when(q < OWNERS)
        def _():
            pltpu.make_async_remote_copy(
                src_ref=p3.at[0], dst_ref=px.at[q], send_sem=s3.at[0], recv_sem=v3.at[q],
                device_id=(f, o), device_id_type=MESH).wait_recv()

        return c

    lax.fori_loop(1, PLANE, back, 0)

    gv_out[...] = g[2]
    for i in range(OWNERS):
        total_out[i] = px[i] + sx[i]

    halos(lambda copy: copy.wait_send())

    def sent(k, c):
        @pl.when((p + k) % PLANE < OWNERS)
        def _():
            pltpu.make_async_remote_copy(
                src_ref=sx.at[0], dst_ref=r1.at[0], send_sem=s1.at[k], recv_sem=v1.at[0],
                device_id=(f, o), device_id_type=MESH).wait_send()

        @pl.when(p < OWNERS)
        def _():
            pltpu.make_async_remote_copy(
                src_ref=p3.at[0], dst_ref=px.at[0], send_sem=s3.at[k], recv_sem=v3.at[0],
                device_id=(f, o), device_id_type=MESH).wait_send()

        return c

    lax.fori_loop(1, PLANE, sent, 0)

    @pl.when(p < OWNERS)
    def _():
        later(lambda k: along(k).wait_send())


def finish(tot, gvs, qts, out_hbm, stage, sem):
    norms = tot[10]
    for h in range(HEADS):
        s = jnp.concatenate(
            [tot[2 * h], tot[2 * h + 1], jnp.broadcast_to(norms[h : h + 1], (16, 128))], axis=0)[:, 0:DH]
        hi = s.astype(BF16)
        lo = (s - hi.astype(F32)).astype(BF16)
        both = nn(jnp.concatenate([hi, lo], axis=0), qts[h * DH : (h + 1) * DH])
        n = both[0:48] + both[48:96]
        den = n[32:33]
        inv = 1.0 / (den + EPS)
        r = n[0:32] * jnp.broadcast_to(inv, (32, TOK))
        ratio = jnp.broadcast_to(den * inv, (16, TOK))
        parts = jnp.concatenate([r, r, ratio], axis=0)
        top = parts.astype(BF16)
        rest = (parts - top.astype(F32)).astype(BF16)
        gv = gvs[h * DH : (h + 1) * DH, 0:80]
        stage[h] = (nn(gv, top) + nn(gv, rest)).astype(BF16)
        pltpu.make_async_copy(stage.at[h], out_hbm.at[h], sem.at[h]).start()
    for h in range(HEADS):
        pltpu.make_async_copy(stage.at[h], out_hbm.at[h], sem.at[h]).wait()


def per_device(latent, conv_weight, conv_bias, proj_weight, embed_weight, embed_bias, qkv_weight):
    width = embed_weight.shape[1]
    lat = jnp.transpose(latent, (1, 3, 2, 0)).reshape(4, 32, 128)
    vmem, anywhere = pl.BlockSpec(memory_space=pltpu.VMEM), pl.BlockSpec(memory_space=pl.ANY)
    dma, vm = pltpu.SemaphoreType.DMA, pltpu.VMEM
    parts = pl.pallas_call(
        kernel,
        out_shape=[
            jax.ShapeDtypeStruct((OWNERS, 16, 128), F32),
            jax.ShapeDtypeStruct((HEADS * DH, 128), BF16),
            jax.ShapeDtypeStruct((HEADS * DH, TOK), BF16),
        ],
        in_specs=[anywhere] * 7,
        out_specs=[vmem] * 3,
        scratch_shapes=[
            vm((4, 32, 128), BF16),
            vm((864, 128), BF16),
            vm((1, 128), F32),
            vm((32, 128), BF16),
            vm((width,), F32),
            vm((3, 2, 4, 32, 128), BF16),
            vm((3, HEADS * DH, width), BF16),
            vm((128, width), BF16),
            vm((3, HEADS * DH, 128), BF16),
            vm((128, 896), BF16),
            vm((896, TOK), BF16),
            vm((128, TOK), BF16),
            vm((128, TOK), BF16),
            vm((TOK, TOK), BF16),
            vm((HEADS * DH, TOK), BF16),
            vm((OWNERS, 16, 128), F32),
            vm((PLANE, 16, 128), F32),
            vm((DEPTH, 16, 128), F32),
            vm((16, 128), F32),
            vm((PLANE, 16, 128), F32),
            vm((OWNERS, 16, 128), F32),
            dma((7,)), dma((5,)), dma((3, 2)), dma((3, 2)),
            dma((PLANE,)), dma((PLANE,)), dma((DEPTH,)), dma((DEPTH,)), dma((PLANE,)), dma((PLANE,)),
            pltpu.SemaphoreType.REGULAR((3,)), pltpu.SemaphoreType.REGULAR((3,)),
        ],
        compiler_params=pltpu.CompilerParams(collective_id=0, has_side_effects=True, vmem_limit_bytes=40 << 20),
    )(*(pltpu.with_memory_space_constraint(v, pltpu.HBM) for v in (
        lat, conv_weight.reshape(864, 128), conv_bias.reshape(1, 128), jnp.transpose(proj_weight),
        embed_weight, embed_bias, jnp.transpose(qkv_weight, (0, 2, 1)),
    )))
    out = pl.pallas_call(
        finish,
        out_shape=jax.ShapeDtypeStruct((HEADS, DH, TOK), BF16),
        in_specs=[vmem] * 3,
        out_specs=anywhere,
        scratch_shapes=[
            vm((HEADS, DH, TOK), BF16), dma((HEADS,)),
        ],
        compiler_params=pltpu.CompilerParams(vmem_limit_bytes=16 << 20),
    )(*parts)
    return jnp.transpose(out.reshape(HEADS * DH, TOK))


def solution(mesh):
    return jax.shard_map(
        per_device,
        mesh=mesh,
        in_specs=(P(None, "tp", None, "seq"), P(), P(), P(), P(), P(), P(None, None, "tp")),
        out_specs=P("seq", "tp"),
        check_vma=False,
    )
```

```python
import functools

import jax
import jax.numpy as jnp
from jax import lax
from jax.experimental import pallas as pl
from jax.experimental.pallas import tpu as pltpu
from jax.sharding import PartitionSpec as P

MESH = pl.DeviceIdType.MESH
F32 = jnp.float32
BF16 = jnp.bfloat16
DH = 112
HEADS = 5
PLANE = 16
DEPTH = 8
OWNERS = 11
NF = PLANE * DEPTH
TOK = 1024
EPS = 1e-6


def nt(a, b):
    return lax.dot_general(a, b, (((1,), (1,)), ((), ())), preferred_element_type=F32)


def nn(a, b):
    return lax.dot_general(a, b, (((1,), (0,)), ((), ())), preferred_element_type=F32)


def three(value):
    hi = value.astype(BF16).astype(F32)
    rest = value - hi
    mid = rest.astype(BF16).astype(F32)
    return hi, mid, (rest - mid).astype(BF16).astype(F32)


def rows_of(parts, rows, width):
    index = lax.broadcasted_iota(jnp.int32, (rows, width), 0)
    out = jnp.zeros((rows, width), F32)
    for i, part in enumerate(parts):
        out = jnp.where(index == i, jnp.broadcast_to(part, (rows, width)), out)
    return out


def kernel(
    lat_hbm, cw_hbm, cb_hbm, pw_hbm, ew_hbm, eb_hbm, w_hbm, total_out, gv_out, qt,
    lat, cw, cb, pw, eb, frames, w, ea, g, cwt, pat, maug, qaug, perm, kt, acc, sx, r1, rz, tz, p3, px,
    ls, hs, hr, ws, s1, v1, s2, v2, s3, v3, tok, ztok,
):
    f = lax.axis_index("seq")
    t = lax.axis_index("tp")
    z, p = f // PLANE, f % PLANE
    o = 1 - t
    x, y = p // 4, p % 4

    barrier = pltpu.get_barrier_semaphore()

    def near(act):
        for ok, seq in ((y > 0, f - 1), (y < 3, f + 1), (x > 0, f - 4), (x < 3, f + 4)):
            pl.when(ok)(functools.partial(act, seq))

    def ahead(step, act, back=True):
        if back:
            pl.when(z >= step)(functools.partial(act, f - step * PLANE))
        if back != "only":
            pl.when(z < DEPTH - step)(functools.partial(act, f + step * PLANE))

    def at_least(value, least, top):
        return (value + top + 1 - least) // (top + 1)

    around = at_least(y, 1, 3) + at_least(3 - y, 1, 3) + at_least(x, 1, 3) + at_least(3 - x, 1, 3)

    def planes(step):
        return at_least(z, step, 7) + at_least(7 - z, step, 7)

    def signal(sem, seq, core):
        pl.semaphore_signal(sem, inc=1, device_id=(seq, core), device_id_type=MESH)

    signal(barrier, f, o)
    for ok, seq in ((f > 0, f - 1), (f < NF - 1, f + 1)):
        @pl.when(ok)
        def _():
            signal(barrier, seq, t)
            signal(barrier, seq, o)

    near(lambda seq: signal(barrier, seq, t))
    ahead(1, lambda seq: signal(barrier, seq, t))

    def load(src, dst, i):
        return pltpu.make_async_copy(src, dst, ls.at[i])

    loads = [
        load(lat_hbm, lat, 0), load(eb_hbm, eb, 1), load(ew_hbm, ea.at[0:32], 2), load(ew_hbm, ea.at[32:64], 3),
        load(cw_hbm, cw, 4), load(cb_hbm, cb, 5), load(pw_hbm, pw, 6),
    ]
    for copy in loads:
        copy.start()

    def wcopy(i, half):
        rows = pl.ds(half * 288, 288 - 16 * half)
        return pltpu.make_async_copy(w_hbm.at[i, rows], w.at[i, rows], ws.at[i, half])

    for i in (1, 2, 0):
        for half in range(2):
            wcopy(i, half).start()

    loads[0].wait()
    frames[1, t] = lat[...]

    width = ea.shape[1]
    loads[1].wait()
    bias = three(eb[...].reshape(1, width))
    ea[64:80] = rows_of(bias + bias, 16, width).astype(BF16)
    ea[80:128] = jnp.zeros((48, width), BF16)

    loads[4].wait()
    loads[5].wait()
    wide = jnp.concatenate([cw[...].astype(F32), rows_of(three(cb[...]), 32, 128)], axis=0)
    cwt[...] = wide.T.astype(BF16)
    pat[864:896] = jnp.ones((32, TOK), BF16)

    pl.semaphore_wait(barrier, 1 + 2 * at_least(f, 1, NF - 1) + 2 * at_least(NF - 1 - f, 1, NF - 1) + around + planes(1))

    def halo(i):
        slot, step, core = ((1, 0, o), (0, 1, t), (0, 1, o), (2, -1, t), (2, -1, o))[i]
        return pltpu.make_async_remote_copy(
            src_ref=lat, dst_ref=frames.at[slot, t], send_sem=hs.at[i], recv_sem=hr.at[slot, t],
            device_id=((f + step + NF) % NF, core), device_id_type=MESH)

    def halos(act):
        act(halo(0))

        @pl.when(f < NF - 1)
        def _():
            act(halo(1))
            act(halo(2))

        @pl.when(f > 0)
        def _():
            act(halo(3))
            act(halo(4))

    halos(lambda copy: copy.start())
    near(lambda seq: signal(tok.at[0], seq, t))
    ahead(1, lambda seq: signal(ztok.at[0], seq, t))

    lane = lax.broadcasted_iota(jnp.int32, (HEADS * DH, 128), 1)
    low = ((lane >= 32) & (lane < 64)) | (lane >= 67)

    loads[2].wait()
    loads[3].wait()
    loads[6].wait()

    def fold(i, c):
        wcopy(i, 0).wait()
        wcopy(i, 1).wait()
        full = nt(w[i], ea[...])
        hi = full.astype(BF16).astype(F32)
        g[i] = jnp.where(low, full - hi, hi).astype(BF16)
        return c

    fold(1, 0)

    pl.semaphore_wait(tok.at[0], around)
    floor = z * PLANE
    signal(tok.at[1], floor + x * 4 + (y + 2) % 4, t)
    signal(tok.at[1], floor + (p + 8) % PLANE, t)

    def fill(i, c):
        target = lax.broadcasted_iota(jnp.int32, (128, TOK), 1)
        source = lax.broadcasted_iota(jnp.int32, (128, TOK), 0)
        hit = ((target & 7) == i) & ((target >> 3) == source)
        perm[pl.ds(pl.multiple_of(i * 128, 128), 128)] = jnp.where(hit, 1.0, 0.0).astype(BF16)
        return c

    lax.fori_loop(0, 8, fill, 0)
    sx[...] = jnp.zeros_like(sx)

    def arrived(slot, core):
        pltpu.make_async_remote_copy(
            src_ref=lat, dst_ref=frames.at[slot, core], send_sem=hs.at[0], recv_sem=hr.at[slot, core],
            device_id=(f, o), device_id_type=MESH).wait_recv()

    row = lax.broadcasted_iota(jnp.int32, (32, TOK), 1) & 127
    none = jnp.zeros((32, 128), BF16)

    def frame(a):
        return jnp.concatenate([frames[a, c // 4, c % 4] for c in range(8)], axis=1).astype(F32)

    def patches(a, image):
        shifted = (
            jnp.where(row == 0, 0.0, pltpu.roll(image, 1, 1)),
            image,
            jnp.where(row == 127, 0.0, pltpu.roll(image, TOK - 1, 1)),
        )
        for b in range(3):
            moved = shifted[b].astype(BF16)
            at = (a * 3 + b) * 96
            pat[at : at + 32] = jnp.concatenate([none, moved[:, : TOK - 128]], axis=1)
            pat[at + 32 : at + 64] = moved
            pat[at + 64 : at + 96] = jnp.concatenate([moved[:, 128:], none], axis=1)

    arrived(1, o)
    here = frame(1)
    patches(1, here)

    @pl.when(f > 0)
    def _():
        arrived(0, t)
        arrived(0, o)

    patches(0, jnp.where(f > 0, frame(0), 0.0))
    acc[...] = nn(cwt[:, 0:576], pat[0:576])

    pl.semaphore_wait(ztok.at[0], planes(1))
    ahead(2, lambda seq: signal(ztok.at[1], seq, t))
    pl.semaphore_wait(tok.at[1], 2)
    for k in range(1, 4):
        signal(tok.at[2], floor + (p + 4 * k) % PLANE, t)

    @pl.when(f < NF - 1)
    def _():
        arrived(2, t)
        arrived(2, o)

    patches(2, jnp.where(f < NF - 1, frame(2), 0.0))
    conv = acc[...] + nn(cwt[:, 576:896], pat[576:896])
    act = (conv / (1.0 + jnp.exp(-conv))).astype(BF16)
    mixed = (nn(pw[...], act) + here).astype(BF16)
    maug[0:32] = mixed
    maug[32:64] = mixed
    maug[64:80] = jnp.ones((16, TOK), BF16)
    maug[80:128] = jnp.zeros((48, TOK), BF16)

    kt[...] = jnp.maximum(nn(g[1], maug[...]), 0.0).astype(BF16)
    plus = maug[32:80]
    for h in range(HEADS):
        s = nt(plus, kt[h * DH : (h + 1) * DH])
        sx[2 * h, :, 0:DH] = s[0:16]
        sx[2 * h + 1, :, 0:DH] = s[16:32]
        sx[10, h : h + 1, 0:DH] = s[32:33]

    pl.semaphore_wait(tok.at[2], 3)

    def along(k):
        return pltpu.make_async_remote_copy(
            src_ref=tz, dst_ref=rz.at[z], send_sem=s2.at[k], recv_sem=v2.at[z],
            device_id=((f + k * PLANE) % NF, t), device_id_type=MESH)

    def later(act):
        for k in (4, 3, 5, 2, 6, 1, 7):
            pl.when(z + k < DEPTH)(functools.partial(act, k))

    peers = sorted(((a, b) for a in range(4) for b in range(4) if a or b), key=lambda c: -sum(min(v, 4 - v) for v in c))

    def across(act):
        for k, (a, b) in enumerate(peers):
            act(k, (x + a) % 4 * 4 + (y + b) % 4)

    def one(k, q):
        @pl.when(q < OWNERS)
        def _():
            pltpu.make_async_remote_copy(
                src_ref=sx.at[q], dst_ref=r1.at[p], send_sem=s1.at[k], recv_sem=v1.at[p],
                device_id=(floor + q, t), device_id_type=MESH).start()

    across(one)

    pl.semaphore_wait(ztok.at[1], planes(2))
    ahead(4, lambda seq: signal(ztok.at[2], seq, t), "only")

    def queries():
        fold(0, 0)
        qaug[...] = nn(maug[...], perm[...]).astype(BF16)
        qt[...] = jnp.maximum(nn(g[0], qaug[...]), 0.0).astype(BF16)

    @pl.when(p < OWNERS)
    def _():
        r1[p] = sx[p]

        def got(k, c):
            q = (p + k) % PLANE
            pltpu.make_async_remote_copy(
                src_ref=sx.at[0], dst_ref=r1.at[q], send_sem=s1.at[0], recv_sem=v1.at[q],
                device_id=(f, o), device_id_type=MESH).wait_recv()
            return c

        lax.fori_loop(1, PLANE, got, 0)
        total = r1[0]
        for i in range(1, PLANE):
            total = total + r1[i]
        tz[...] = total
        pl.when(z < 4)(functools.partial(pl.semaphore_wait, ztok.at[2], 1))
        later(lambda k: along(k).start())
        run = jnp.zeros((16, 128), F32)
        for i in range(PLANE):
            p3[i] = run
            run = run + r1[i]

    @pl.when((p >= OWNERS) & (z < 4))
    def _():
        pl.semaphore_wait(ztok.at[2], 1)

    queries()

    @pl.when(p < OWNERS)
    def _():
        def got(k, c):
            @pl.when(k < z)
            def _():
                pltpu.make_async_remote_copy(
                    src_ref=tz, dst_ref=rz.at[k], send_sem=s2.at[0], recv_sem=v2.at[k],
                    device_id=(f, o), device_id_type=MESH).wait_recv()

            return c

        lax.fori_loop(0, DEPTH - 1, got, 0)
        before = jnp.zeros((16, 128), F32)
        for i in range(DEPTH - 1):
            before = before + jnp.where(i < z, rz[i], 0.0)
        for i in range(PLANE):
            p3[i] = p3[i] + before

        def three_(k, q):
            pltpu.make_async_remote_copy(
                src_ref=p3.at[q], dst_ref=px.at[p], send_sem=s3.at[k], recv_sem=v3.at[p],
                device_id=(floor + q, t), device_id_type=MESH).start()

        across(three_)
        px[p] = p3[p]

    fold(2, 0)
    gv_out[...] = g[2]

    def back(k, c):
        q = (p + k) % PLANE

        @pl.when(q < OWNERS)
        def _():
            pltpu.make_async_remote_copy(
                src_ref=p3.at[0], dst_ref=px.at[q], send_sem=s3.at[0], recv_sem=v3.at[q],
                device_id=(f, o), device_id_type=MESH).wait_recv()

        return c

    lax.fori_loop(1, PLANE, back, 0)

    for i in range(OWNERS):
        total_out[i] = px[i] + sx[i]

    halos(lambda copy: copy.wait_send())

    def sent(k, q):
        @pl.when(q < OWNERS)
        def _():
            pltpu.make_async_remote_copy(
                src_ref=sx.at[0], dst_ref=r1.at[0], send_sem=s1.at[k], recv_sem=v1.at[0],
                device_id=(f, o), device_id_type=MESH).wait_send()

        @pl.when(p < OWNERS)
        def _():
            pltpu.make_async_remote_copy(
                src_ref=p3.at[0], dst_ref=px.at[0], send_sem=s3.at[k], recv_sem=v3.at[0],
                device_id=(f, o), device_id_type=MESH).wait_send()

    across(sent)

    @pl.when(p < OWNERS)
    def _():
        later(lambda k: along(k).wait_send())


def finish(tot, gvs, qts, out_hbm, stage, sem):
    norms = tot[10]
    for h in range(HEADS):
        s = jnp.concatenate(
            [tot[2 * h], tot[2 * h + 1], jnp.broadcast_to(norms[h : h + 1], (16, 128))], axis=0)[:, 0:DH]
        hi = s.astype(BF16)
        lo = (s - hi.astype(F32)).astype(BF16)
        both = nn(jnp.concatenate([hi, lo], axis=0), qts[h * DH : (h + 1) * DH])
        n = both[0:48] + both[48:96]
        den = n[32:33]
        inv = 1.0 / (den + EPS)
        r = n[0:32] * jnp.broadcast_to(inv, (32, TOK))
        ratio = jnp.broadcast_to(den * inv, (16, TOK))
        parts = jnp.concatenate([r, r, ratio], axis=0)
        top = parts.astype(BF16)
        rest = (parts - top.astype(F32)).astype(BF16)
        gv = gvs[h * DH : (h + 1) * DH, 0:80]
        stage[h] = (nn(gv, top) + nn(gv, rest)).astype(BF16)
        pltpu.make_async_copy(stage.at[h], out_hbm.at[h], sem.at[h]).start()
    for h in range(HEADS):
        pltpu.make_async_copy(stage.at[h], out_hbm.at[h], sem.at[h]).wait()


def per_device(latent, conv_weight, conv_bias, proj_weight, embed_weight, embed_bias, qkv_weight):
    width = embed_weight.shape[1]
    lat = jnp.transpose(latent, (1, 3, 2, 0)).reshape(4, 32, 128)
    vmem, anywhere = pl.BlockSpec(memory_space=pltpu.VMEM), pl.BlockSpec(memory_space=pl.ANY)
    dma, vm = pltpu.SemaphoreType.DMA, pltpu.VMEM
    parts = pl.pallas_call(
        kernel,
        out_shape=[
            jax.ShapeDtypeStruct((OWNERS, 16, 128), F32),
            jax.ShapeDtypeStruct((HEADS * DH, 128), BF16),
            jax.ShapeDtypeStruct((HEADS * DH, TOK), BF16),
        ],
        in_specs=[anywhere] * 7,
        out_specs=[vmem] * 3,
        scratch_shapes=[
            vm((4, 32, 128), BF16),
            vm((864, 128), BF16),
            vm((1, 128), F32),
            vm((32, 128), BF16),
            vm((width,), F32),
            vm((3, 2, 4, 32, 128), BF16),
            vm((3, HEADS * DH, width), BF16),
            vm((128, width), BF16),
            vm((3, HEADS * DH, 128), BF16),
            vm((128, 896), BF16),
            vm((896, TOK), BF16),
            vm((128, TOK), BF16),
            vm((128, TOK), BF16),
            vm((TOK, TOK), BF16),
            vm((HEADS * DH, TOK), BF16),
            vm((128, TOK), F32),
            vm((OWNERS, 16, 128), F32),
            vm((PLANE, 16, 128), F32),
            vm((DEPTH, 16, 128), F32),
            vm((16, 128), F32),
            vm((PLANE, 16, 128), F32),
            vm((OWNERS, 16, 128), F32),
            dma((7,)), dma((5,)), dma((3, 2)), dma((3, 2)),
            dma((PLANE,)), dma((PLANE,)), dma((DEPTH,)), dma((DEPTH,)), dma((PLANE,)), dma((PLANE,)),
            pltpu.SemaphoreType.REGULAR((3,)), pltpu.SemaphoreType.REGULAR((3,)),
        ],
        compiler_params=pltpu.CompilerParams(collective_id=0, has_side_effects=True, vmem_limit_bytes=40 << 20),
    )(*(pltpu.with_memory_space_constraint(v, pltpu.HBM) for v in (
        lat, conv_weight.reshape(864, 128), conv_bias.reshape(1, 128), jnp.transpose(proj_weight),
        embed_weight, embed_bias, jnp.transpose(qkv_weight, (0, 2, 1)),
    )))
    out = pl.pallas_call(
        finish,
        out_shape=jax.ShapeDtypeStruct((HEADS, DH, TOK), BF16),
        in_specs=[vmem] * 3,
        out_specs=anywhere,
        scratch_shapes=[
            vm((HEADS, DH, TOK), BF16), dma((HEADS,)),
        ],
        compiler_params=pltpu.CompilerParams(vmem_limit_bytes=16 << 20),
    )(*parts)
    return jnp.transpose(out.reshape(HEADS * DH, TOK))


def solution(mesh):
    return jax.shard_map(
        per_device,
        mesh=mesh,
        in_specs=(P(None, "tp", None, "seq"), P(), P(), P(), P(), P(), P(None, None, "tp")),
        out_specs=P("seq", "tp"),
        check_vma=False,
    )
```

```python
import functools

import jax
import jax.numpy as jnp
from jax import lax
from jax.experimental import pallas as pl
from jax.experimental.pallas import tpu as pltpu
from jax.sharding import PartitionSpec as P

MESH = pl.DeviceIdType.MESH
F32 = jnp.float32
BF16 = jnp.bfloat16
DH = 112
HEADS = 5
PLANE = 16
DEPTH = 8
OWNERS = 11
NF = PLANE * DEPTH
TOK = 1024
EPS = 1e-6


def nt(a, b):
    return lax.dot_general(a, b, (((1,), (1,)), ((), ())), preferred_element_type=F32)


def nn(a, b):
    return lax.dot_general(a, b, (((1,), (0,)), ((), ())), preferred_element_type=F32)


def three(value):
    hi = value.astype(BF16).astype(F32)
    rest = value - hi
    mid = rest.astype(BF16).astype(F32)
    return hi, mid, (rest - mid).astype(BF16).astype(F32)


def rows_of(parts, rows, width):
    index = lax.broadcasted_iota(jnp.int32, (rows, width), 0)
    out = jnp.zeros((rows, width), F32)
    for i, part in enumerate(parts):
        out = jnp.where(index == i, jnp.broadcast_to(part, (rows, width)), out)
    return out


def kernel(
    lat_hbm, cw_hbm, cb_hbm, pw_hbm, ew_hbm, eb_hbm, w_hbm, total_out, gv_out, qt,
    lat, cw, cb, pw, eb, frames, w, ea, g, cwt, pat, maug, qaug, perm, kt, acc, sx, r1, rz, tz, p3, px,
    ls, hs, hr, ws, s1, v1, s2, v2, s3, v3, tok, ztok,
):
    f = lax.axis_index("seq")
    t = lax.axis_index("tp")
    z, p = f // PLANE, f % PLANE
    o = 1 - t
    x, y = p // 4, p % 4

    barrier = pltpu.get_barrier_semaphore()

    def near(act):
        for ok, seq in ((y > 0, f - 1), (y < 3, f + 1), (x > 0, f - 4), (x < 3, f + 4)):
            pl.when(ok)(functools.partial(act, seq))

    def ahead(step, act, back=True):
        if back:
            pl.when(z >= step)(functools.partial(act, f - step * PLANE))
        if back != "only":
            pl.when(z < DEPTH - step)(functools.partial(act, f + step * PLANE))

    def at_least(value, least, top):
        return (value + top + 1 - least) // (top + 1)

    def owns(q):
        return (q != 5) & (q != 6) & (q != 9) & (q != 10) & (q != 15)

    def slice_of(q):
        return q - at_least(q, 6, 15) - at_least(q, 7, 15) - at_least(q, 10, 15) - at_least(q, 11, 15)

    around = at_least(y, 1, 3) + at_least(3 - y, 1, 3) + at_least(x, 1, 3) + at_least(3 - x, 1, 3)

    def planes(step):
        return at_least(z, step, 7) + at_least(7 - z, step, 7)

    def signal(sem, seq, core):
        pl.semaphore_signal(sem, inc=1, device_id=(seq, core), device_id_type=MESH)

    signal(barrier, f, o)
    for ok, seq in ((f > 0, f - 1), (f < NF - 1, f + 1)):
        @pl.when(ok)
        def _():
            signal(barrier, seq, t)
            signal(barrier, seq, o)

    near(lambda seq: signal(barrier, seq, t))
    ahead(1, lambda seq: signal(barrier, seq, t))

    def load(src, dst, i):
        return pltpu.make_async_copy(src, dst, ls.at[i])

    loads = [
        load(lat_hbm, lat, 0), load(eb_hbm, eb, 1), load(ew_hbm, ea.at[0:32], 2), load(ew_hbm, ea.at[32:64], 3),
        load(cw_hbm, cw, 4), load(cb_hbm, cb, 5), load(pw_hbm, pw, 6),
    ]
    for copy in loads:
        copy.start()

    def wcopy(i, half):
        rows = pl.ds(half * 288, 288 - 16 * half)
        return pltpu.make_async_copy(w_hbm.at[i, rows], w.at[i, rows], ws.at[i, half])

    for i in (1, 2, 0):
        for half in range(2):
            wcopy(i, half).start()

    loads[0].wait()
    frames[1, t] = lat[...]

    pl.semaphore_wait(barrier, 1 + 2 * at_least(f, 1, NF - 1) + 2 * at_least(NF - 1 - f, 1, NF - 1) + around + planes(1))

    def halo(i):
        slot, step, core = ((1, 0, o), (0, 1, t), (0, 1, o), (2, -1, t), (2, -1, o))[i]
        return pltpu.make_async_remote_copy(
            src_ref=lat, dst_ref=frames.at[slot, t], send_sem=hs.at[i], recv_sem=hr.at[slot, t],
            device_id=((f + step + NF) % NF, core), device_id_type=MESH)

    def halos(act):
        @pl.when(f < NF - 1)
        def _():
            act(halo(1))
            act(halo(2))

        @pl.when(f > 0)
        def _():
            act(halo(3))
            act(halo(4))

        act(halo(0))

    halos(lambda copy: copy.start())
    near(lambda seq: signal(tok.at[0], seq, t))
    ahead(1, lambda seq: signal(ztok.at[0], seq, t))

    width = ea.shape[1]
    loads[1].wait()
    bias = three(eb[...].reshape(1, width))
    ea[64:80] = rows_of(bias + bias, 16, width).astype(BF16)
    ea[80:128] = jnp.zeros((48, width), BF16)

    loads[4].wait()
    loads[5].wait()
    bias_rows = rows_of(three(cb[...]), 32, 128)
    for a in range(3):
        wide = [cw[a * 288 : a * 288 + 288].astype(F32), bias_rows if a == 1 else jnp.zeros((32, 128), F32)]
        cwt[a] = jnp.concatenate(wide, axis=0).T.astype(BF16)
        pat[a, 288:320] = jnp.ones((32, TOK), BF16)

    lane = lax.broadcasted_iota(jnp.int32, (HEADS * DH, 128), 1)
    low = ((lane >= 32) & (lane < 64)) | (lane >= 67)

    loads[2].wait()
    loads[3].wait()
    loads[6].wait()

    def fold(i, c):
        wcopy(i, 0).wait()
        wcopy(i, 1).wait()
        full = nt(w[i], ea[...])
        hi = full.astype(BF16).astype(F32)
        g[i] = jnp.where(low, full - hi, hi).astype(BF16)
        return c

    fold(1, 0)

    pl.semaphore_wait(tok.at[0], around)
    floor = z * PLANE
    signal(tok.at[1], floor + x * 4 + (y + 2) % 4, t)
    signal(tok.at[1], floor + (p + 8) % PLANE, t)

    def fill(i, c):
        target = lax.broadcasted_iota(jnp.int32, (128, TOK), 1)
        source = lax.broadcasted_iota(jnp.int32, (128, TOK), 0)
        hit = ((target & 7) == i) & ((target >> 3) == source)
        perm[pl.ds(pl.multiple_of(i * 128, 128), 128)] = jnp.where(hit, 1.0, 0.0).astype(BF16)
        return c

    lax.fori_loop(0, 8, fill, 0)
    sx[...] = jnp.zeros_like(sx)

    def arrived(slot, core):
        pltpu.make_async_remote_copy(
            src_ref=lat, dst_ref=frames.at[slot, core], send_sem=hs.at[0], recv_sem=hr.at[slot, core],
            device_id=(f, o), device_id_type=MESH).wait_recv()

    row = lax.broadcasted_iota(jnp.int32, (32, TOK), 1) & 127
    none = jnp.zeros((32, 128), BF16)

    def frame(a):
        return jnp.concatenate([frames[a, c // 4, c % 4] for c in range(8)], axis=1).astype(F32)

    def patches(a, image):
        shifted = (
            jnp.where(row == 0, 0.0, pltpu.roll(image, 1, 1)),
            image,
            jnp.where(row == 127, 0.0, pltpu.roll(image, TOK - 1, 1)),
        )
        for b in range(3):
            moved = shifted[b].astype(BF16)
            at = b * 96
            pat[a, at : at + 32] = jnp.concatenate([none, moved[:, : TOK - 128]], axis=1)
            pat[a, at + 32 : at + 64] = moved
            pat[a, at + 64 : at + 96] = jnp.concatenate([moved[:, 128:], none], axis=1)

    arrived(1, o)
    here = frame(1)
    patches(1, here)

    pl.semaphore_wait(ztok.at[0], planes(1))
    ahead(2, lambda seq: signal(ztok.at[1], seq, t))
    pl.semaphore_wait(tok.at[1], 2)
    for k in range(1, 4):
        signal(tok.at[2], floor + (p + 4 * k) % PLANE, t)

    last = jnp.where(y == 0, 0, 2)

    def frame_of(a):
        columns = [frames[a, c // 4, c % 4] for c in range(8)]
        image = jnp.concatenate(columns, axis=1).astype(F32)
        return jnp.where(f + a - 1 < 0, 0.0, jnp.where(f + a - 1 > NF - 1, 0.0, image))

    def come(a):
        @pl.when((f + a - 1 >= 0) & (f + a - 1 < NF))
        def _():
            arrived(a, t)
            arrived(a, o)

    come(2 - last)
    patches(2 - last, frame_of(2 - last))
    acc[...] = nn(cwt[1], pat[1]) + nn(cwt[2 - last], pat[2 - last])
    come(last)
    patches(last, frame_of(last))
    @pl.when(z >= 4)
    def _():
        pl.semaphore_wait(ztok.at[1], planes(2))
        signal(ztok.at[2], f - 4 * PLANE, t)

    conv = acc[...] + nn(cwt[last], pat[last])
    act = (conv / (1.0 + jnp.exp(-conv))).astype(BF16)
    mixed = (nn(pw[...], act) + here).astype(BF16)
    maug[0:32] = mixed
    maug[32:64] = mixed
    maug[64:80] = jnp.ones((16, TOK), BF16)
    maug[80:128] = jnp.zeros((48, TOK), BF16)

    kt[...] = jnp.maximum(nn(g[1], maug[...]), 0.0).astype(BF16)
    plus = maug[32:80]
    for h in range(HEADS):
        s = nt(plus, kt[h * DH : (h + 1) * DH])
        sx[2 * h, :, 0:DH] = s[0:16]
        sx[2 * h + 1, :, 0:DH] = s[16:32]
        sx[10, h : h + 1, 0:DH] = s[32:33]

    pl.semaphore_wait(tok.at[2], 3)

    def along(k):
        return pltpu.make_async_remote_copy(
            src_ref=tz, dst_ref=rz.at[z], send_sem=s2.at[k], recv_sem=v2.at[z],
            device_id=((f + k * PLANE) % NF, t), device_id_type=MESH)

    def later(act, steps=range(1, DEPTH)):
        for k in steps:
            pl.when(z + k < DEPTH)(functools.partial(act, k))

    peers = sorted(((a, b) for a in range(4) for b in range(4) if a or b), key=lambda c: -sum(min(v, 4 - v) for v in c))

    def across(act):
        for k, (a, b) in enumerate(peers):
            act(k, (x + a) % 4 * 4 + (y + b) % 4)

    def one(k, q):
        @pl.when(owns(q))
        def _():
            pltpu.make_async_remote_copy(
                src_ref=sx.at[slice_of(q)], dst_ref=r1.at[p], send_sem=s1.at[k], recv_sem=v1.at[p],
                device_id=(floor + q, t), device_id_type=MESH).start()

    across(one)

    @pl.when(z < 4)
    def _():
        pl.semaphore_wait(ztok.at[1], planes(2))


    def queries():
        fold(0, 0)
        qaug[...] = nn(maug[...], perm[...]).astype(BF16)
        qt[...] = jnp.maximum(nn(g[0], qaug[...]), 0.0).astype(BF16)

    @pl.when(owns(p))
    def _():
        r1[p] = sx[slice_of(p)]

        def got(k, c):
            q = (p + k) % PLANE
            pltpu.make_async_remote_copy(
                src_ref=sx.at[0], dst_ref=r1.at[q], send_sem=s1.at[0], recv_sem=v1.at[q],
                device_id=(f, o), device_id_type=MESH).wait_recv()
            return c

        lax.fori_loop(1, PLANE, got, 0)
        total = r1[0]
        for i in range(1, PLANE):
            total = total + r1[i]
        tz[...] = total
        later(lambda k: along(k).start(), (4, 3, 2, 1))
        pl.when(z < 4)(functools.partial(pl.semaphore_wait, ztok.at[2], 1))
        later(lambda k: along(k).start(), (5, 6, 7))
        run = jnp.zeros((16, 128), F32)
        for i in range(PLANE):
            p3[i] = run
            run = run + r1[i]

    @pl.when(jnp.logical_not(owns(p)) & (z < 4))
    def _():
        pl.semaphore_wait(ztok.at[2], 1)

    @pl.when(owns(p))
    def _():
        def got(k, c):
            @pl.when(k < z)
            def _():
                pltpu.make_async_remote_copy(
                    src_ref=tz, dst_ref=rz.at[k], send_sem=s2.at[0], recv_sem=v2.at[k],
                    device_id=(f, o), device_id_type=MESH).wait_recv()

            return c

        lax.fori_loop(0, DEPTH - 1, got, 0)
        before = jnp.zeros((16, 128), F32)
        for i in range(DEPTH - 1):
            before = before + jnp.where(i < z, rz[i], 0.0)
        for i in range(PLANE):
            p3[i] = p3[i] + before

        def three_(k, q):
            pltpu.make_async_remote_copy(
                src_ref=p3.at[q], dst_ref=px.at[slice_of(p)], send_sem=s3.at[k], recv_sem=v3.at[slice_of(p)],
                device_id=(floor + q, t), device_id_type=MESH).start()

        across(three_)
        px[slice_of(p)] = p3[p]

    fold(2, 0)
    gv_out[...] = g[2]
    queries()

    def back(k, q):
        @pl.when(owns(q))
        def _():
            pltpu.make_async_remote_copy(
                src_ref=p3.at[0], dst_ref=px.at[slice_of(q)], send_sem=s3.at[0], recv_sem=v3.at[slice_of(q)],
                device_id=(f, o), device_id_type=MESH).wait_recv()

    across(back)

    for i in range(OWNERS):
        total_out[i] = px[i] + sx[i]

    halos(lambda copy: copy.wait_send())

    def sent(k, q):
        @pl.when(owns(q))
        def _():
            pltpu.make_async_remote_copy(
                src_ref=sx.at[0], dst_ref=r1.at[0], send_sem=s1.at[k], recv_sem=v1.at[0],
                device_id=(f, o), device_id_type=MESH).wait_send()

        @pl.when(owns(p))
        def _():
            pltpu.make_async_remote_copy(
                src_ref=p3.at[0], dst_ref=px.at[0], send_sem=s3.at[k], recv_sem=v3.at[0],
                device_id=(f, o), device_id_type=MESH).wait_send()

    across(sent)

    @pl.when(owns(p))
    def _():
        later(lambda k: along(k).wait_send())


def finish(tot, gvs, qts, out_hbm, stage, sem):
    norms = tot[10]
    for h in range(HEADS):
        s = jnp.concatenate(
            [tot[2 * h], tot[2 * h + 1], jnp.broadcast_to(norms[h : h + 1], (16, 128))], axis=0)[:, 0:DH]
        hi = s.astype(BF16)
        lo = (s - hi.astype(F32)).astype(BF16)
        both = nn(jnp.concatenate([hi, lo], axis=0), qts[h * DH : (h + 1) * DH])
        n = both[0:48] + both[48:96]
        den = n[32:33]
        inv = 1.0 / (den + EPS)
        r = n[0:32] * jnp.broadcast_to(inv, (32, TOK))
        ratio = jnp.broadcast_to(den * inv, (16, TOK))
        parts = jnp.concatenate([r, r, ratio, r, ratio], axis=0)
        top = parts.astype(BF16)
        rest = (parts - top.astype(F32)).astype(BF16)
        gv = gvs[h * DH : (h + 1) * DH]
        stage[h] = nn(jnp.concatenate([gv, gv], axis=1), jnp.concatenate([top, rest], axis=0)).astype(BF16)
        pltpu.make_async_copy(stage.at[h], out_hbm.at[h], sem.at[h]).start()
    for h in range(HEADS):
        pltpu.make_async_copy(stage.at[h], out_hbm.at[h], sem.at[h]).wait()


def per_device(latent, conv_weight, conv_bias, proj_weight, embed_weight, embed_bias, qkv_weight):
    width = embed_weight.shape[1]
    lat = jnp.transpose(latent, (1, 3, 2, 0)).reshape(4, 32, 128)
    vmem, anywhere = pl.BlockSpec(memory_space=pltpu.VMEM), pl.BlockSpec(memory_space=pl.ANY)
    dma, vm = pltpu.SemaphoreType.DMA, pltpu.VMEM
    parts = pl.pallas_call(
        kernel,
        out_shape=[
            jax.ShapeDtypeStruct((OWNERS, 16, 128), F32),
            jax.ShapeDtypeStruct((HEADS * DH, 128), BF16),
            jax.ShapeDtypeStruct((HEADS * DH, TOK), BF16),
        ],
        in_specs=[anywhere] * 7,
        out_specs=[vmem] * 3,
        scratch_shapes=[
            vm((4, 32, 128), BF16),
            vm((864, 128), BF16),
            vm((1, 128), F32),
            vm((32, 128), BF16),
            vm((width,), F32),
            vm((3, 2, 4, 32, 128), BF16),
            vm((3, HEADS * DH, width), BF16),
            vm((128, width), BF16),
            vm((3, HEADS * DH, 128), BF16),
            vm((3, 128, 320), BF16),
            vm((3, 320, TOK), BF16),
            vm((128, TOK), BF16),
            vm((128, TOK), BF16),
            vm((TOK, TOK), BF16),
            vm((HEADS * DH, TOK), BF16),
            vm((128, TOK), F32),
            vm((OWNERS, 16, 128), F32),
            vm((PLANE, 16, 128), F32),
            vm((DEPTH, 16, 128), F32),
            vm((16, 128), F32),
            vm((PLANE, 16, 128), F32),
            vm((OWNERS, 16, 128), F32),
            dma((7,)), dma((5,)), dma((3, 2)), dma((3, 2)),
            dma((PLANE,)), dma((PLANE,)), dma((DEPTH,)), dma((DEPTH,)), dma((PLANE,)), dma((PLANE,)),
            pltpu.SemaphoreType.REGULAR((3,)), pltpu.SemaphoreType.REGULAR((3,)),
        ],
        compiler_params=pltpu.CompilerParams(collective_id=0, has_side_effects=True, vmem_limit_bytes=40 << 20),
    )(*(pltpu.with_memory_space_constraint(v, pltpu.HBM) for v in (
        lat, conv_weight.reshape(864, 128), conv_bias.reshape(1, 128), jnp.transpose(proj_weight),
        embed_weight, embed_bias, jnp.transpose(qkv_weight, (0, 2, 1)),
    )))
    out = pl.pallas_call(
        finish,
        out_shape=jax.ShapeDtypeStruct((HEADS, DH, TOK), BF16),
        in_specs=[vmem] * 3,
        out_specs=anywhere,
        scratch_shapes=[
            vm((HEADS, DH, TOK), BF16), dma((HEADS,)),
        ],
        compiler_params=pltpu.CompilerParams(vmem_limit_bytes=16 << 20),
    )(*parts)
    return jnp.transpose(out.reshape(HEADS * DH, TOK))


def solution(mesh):
    return jax.shard_map(
        per_device,
        mesh=mesh,
        in_specs=(P(None, "tp", None, "seq"), P(), P(), P(), P(), P(), P(None, None, "tp")),
        out_specs=P("seq", "tp"),
        check_vma=False,
    )
```
